32 devices in a mesh: groups: 2 (over x), roll: 4 (over y, core), rows: 4 (over z).
Axes of the slice: x: 2, y: 2, z: 4, core: 2. Of those that a mesh axis runs over, the one named last changes fastest.
Arguments:
- latent_slabs: bfloat16 [16, 3, 32, 8, 16], P(('groups', 'roll'), None, 'rows'), parts along dimension 0, may hold values from -18 to 18, as said below
- prior_latents: bfloat16 [16, 2, 32, 8, 16], P(('groups', 'roll'), None, 'rows'), parts along dimension 0, may hold values from -6 to 6
- prior_features: bfloat16 [16, 2, 32, 8, 512], P(('groups', 'roll'), None, 'rows'), parts along dimension 0, may hold values from -6 to 6
- lengths: int32 [16], P(('groups', 'roll')), parts along dimension 0, may hold values from 1 to 3
- starts: int32 [16], P(('groups', 'roll')), parts along dimension 0, may hold values from 0 to 6, as said below
- move_plan: int32 [16], P(('groups', 'roll')), parts along dimension 0, may hold values from -1 to 3, as said below
- entry_weight: bfloat16 [432, 512], replicated, may hold values from -0.3125 to 0.3125
- block_weight: bfloat16 [13824, 512], P(None, ('roll', 'rows')), may hold values from -0.0546875 to 0.0546875
- norm_gain: float32 [512], replicated, may hold values from 0.25 to 1.75
- norm_shift: float32 [512], replicated, may hold values from -1.2 to 1.2
Outputs:
- decoded: bfloat16 [16, 3, 32, 8, 512], P(('groups', 'roll'), None, 'rows'), parts along dimension 0
The draws below stay inside these ranges and needn't reach their ends.
There are 2 independent parts, one for each index of `groups`. The reference program is written for one: setup_inputs(seed, part) draws one part's arguments, and reference() takes and returns one part's arrays. A program takes and returns all parts, laid end to end along the dimension named above; an argument that names none is the same for every part. Nothing has to cross between parts.
Inputs may be any that keep to these rules, and one draw needn't show every extreme that they name: `latent_slabs`: normal or uniform values times a scale that varies over the rows. `starts`: multiples of 3. `move_plan`: A value d * 1 + c names compute slot c of roll index d. Every compute slot of the part is named by exactly one slab, and the slabs held by one roll index name at most 1 slots of any one roll index.
All inputs are finite; a program needn't handle non-finite values.
Results may differ from the reference program's by a relative error of at most 0.0023.
Values may be sent and summed in bfloat16 or wider, within the bound.
A program may use at most 128 MiB of HBM per device.

```python
import jax
import jax.numpy as jnp
from jax import lax

LAT = 16
FEAT = 512
GROUPS = 32
FRAMES = 3
COLS = 8
ROLL_DEV = 2
CAP = 1
SLABS = 8
HEIGHT = 32
N_ROLL = 4


def draw_latent_slabs(key, part):
    shape_full = (SLABS, FRAMES, HEIGHT, COLS, LAT)
    height_pos = jnp.arange(HEIGHT, dtype=jnp.float32) / max(HEIGHT - 1, 1)
    values = jnp.clip(jax.random.normal(jax.random.fold_in(key, 3), shape_full, jnp.float32), -6.0, 6.0)
    rising = jnp.exp(jnp.log(3.0) * height_pos)
    return (values * rising[None, None, :, None, None]).astype(jnp.bfloat16)


def draw_starts(key, part):
    return (FRAMES * jax.random.randint(jax.random.fold_in(key, 5), (SLABS,), 0, 3)).astype(jnp.int32)


def draw_move_plan(key, part):
    owners = jnp.arange(SLABS) // ROLL_DEV
    leaning = jax.random.randint(jax.random.fold_in(key, 7), (N_ROLL,), 0, 4)
    favored = jax.random.randint(jax.random.fold_in(key, 8), (), 0, N_ROLL)
    leaning = jnp.where(jnp.arange(N_ROLL) == favored, 16, leaning)
    jitter = jax.random.randint(jax.random.fold_in(key, 9), (SLABS,), 0, 64)
    scores = (jitter + 48 * leaning[owners]) * SLABS + jnp.arange(SLABS)
    ranking = jnp.argsort(-scores)
    chosen = jnp.zeros((SLABS,), jnp.int32).at[ranking[:CAP * N_ROLL]].set(1)
    counter = jnp.cumsum(chosen) - 1
    return jnp.where(chosen > 0, counter % N_ROLL * CAP + counter // N_ROLL, -1).astype(jnp.int32)


def touch_ends(entries, stream_key, least, largest):
    longest = entries.shape.index(max(entries.shape))
    spots = []
    for shift in (0, 1):
        where = [jax.random.randint(jax.random.fold_in(stream_key, axis), (), 0, length) for axis, length in enumerate(entries.shape)]
        where[longest] = (where[longest] + shift) % entries.shape[longest]
        spots.append(tuple(where))
    return entries.at[spots[0]].set(least).at[spots[1]].set(largest)


def steps_of(rng, dims, cuts, least, top_value):
    level, own = 1.0, jax.random.fold_in(rng, 6)
    for position, blocks in cuts:
        steps = jnp.exp(jax.random.uniform(jax.random.fold_in(own, position), (blocks,), jnp.float32, least / len(cuts), top_value / len(cuts)))
        level = level * jnp.repeat(steps, dims[position] // blocks).reshape([-1 if axis == position else 1 for axis in range(len(dims))])
    return level


def normal_values(stream_key, dims, spread, bound, pieces=(), held_as=jnp.bfloat16):
    loudness = steps_of(stream_key, dims, pieces, -0.22, 0.18) if pieces else 1.0
    result = jax.random.normal(stream_key, dims, jnp.float32) * spread * loudness
    return jnp.minimum(jnp.maximum(result, -bound), bound).astype(held_as)


def setup_inputs(seed: int = 0, part: int = 0) -> dict:
    key_of = jax.random.split(jax.random.key(seed), 11)
    part_splits = jax.random.split(jax.random.fold_in(key_of[10], part), 11)
    latent_slabs = draw_latent_slabs(jax.random.fold_in(jax.random.fold_in(key_of[10], part), 71), part)
    prior_latents = normal_values(part_splits[1], (SLABS, 2, HEIGHT, COLS, LAT), 1.0, 6.0, ((0, 4), (2, 4)))
    prior_features = normal_values(part_splits[2], (SLABS, 2, HEIGHT, COLS, FEAT), 1.0, 6.0, ((0, 4), (2, 4)))
    lengths = touch_ends(jax.random.randint(part_splits[3], (SLABS,), 1, FRAMES + 1), jax.random.fold_in(part_splits[3], 1), 1, FRAMES).astype(jnp.int32)
    starts = draw_starts(jax.random.fold_in(jax.random.fold_in(key_of[10], part), 71), part)
    move_plan = draw_move_plan(jax.random.fold_in(jax.random.fold_in(key_of[10], part), 71), part)
    entry_weight = normal_values(key_of[6], (27 * LAT, FEAT), (27 * LAT) ** -0.5, 0.3125)
    block_weight = normal_values(key_of[7], (27 * FEAT, FEAT), (27 * FEAT) ** -0.5, 0.0546875, ((1, 16),))
    norm_gain = jnp.clip(1.0 + 0.15 * jax.random.normal(key_of[8], (FEAT,), jnp.float32), 0.25, 1.75)
    norm_shift = normal_values(key_of[9], (FEAT,), 0.3, 1.2, (), jnp.float32)
    return {"latent_slabs": latent_slabs, "prior_latents": prior_latents, "prior_features": prior_features, "lengths": lengths, "starts": starts, "move_plan": move_plan, "entry_weight": entry_weight, "block_weight": block_weight, "norm_gain": norm_gain, "norm_shift": norm_shift}


EPSILON = 1e-06

def convolve(extended, weights):
    frames = extended.shape[0] - 2
    height = extended.shape[1] - 2
    widths = extended.shape[2] - 2
    channels = extended.shape[3]
    accumulated = jnp.zeros((frames * height * widths, weights.shape[1]), jnp.float32)
    for tap_index in range(27):
        step_t = tap_index // 9
        step_h = tap_index // 3 % 3
        step_w = tap_index % 3
        window = extended[step_t:step_t + frames, step_h:step_h + height, step_w:step_w + widths, :]
        accumulated = accumulated + jnp.dot(window.reshape(-1, channels), weights[tap_index * channels:(tap_index + 1) * channels], preferred_element_type=jnp.float32, precision=lax.Precision.HIGHEST)
    return accumulated.reshape(frames, height, widths, weights.shape[1])

def reference(latent_slabs, prior_latents, prior_features, lengths, starts, move_plan, entry_weight, block_weight, norm_gain, norm_shift):
    entry_full = entry_weight.astype(jnp.float32)
    block_full = block_weight.astype(jnp.float32)
    gain_vector = norm_gain.astype(jnp.float32)
    shift_vector = norm_shift.astype(jnp.float32)

    def decode_slab(element):
        latent, prior_lat, prior_feat, length, first_frame, target = element
        cached = first_frame > 0
        prior_lat = jnp.where(cached, prior_lat, jnp.zeros_like(prior_lat))
        prior_feat = jnp.where(cached, prior_feat, jnp.zeros_like(prior_feat))
        stacked = jnp.concatenate([prior_lat, latent], axis=0).astype(jnp.float32)
        hidden = convolve(jnp.pad(stacked, ((0, 0), (1, 1), (1, 1), (0, 0))), entry_full)
        frames, height, widths, features = hidden.shape
        grouped = hidden.reshape(frames, height, widths, GROUPS, features // GROUPS)
        group_mean = lax.optimization_barrier(jnp.mean(grouped, axis=(1, 2, 4)))
        square_mean = lax.optimization_barrier(jnp.mean(grouped * grouped, axis=(1, 2, 4)))
        scaled = lax.rsqrt(square_mean - group_mean * group_mean + EPSILON)
        normed = ((grouped - group_mean[:, None, None, :, None]) * scaled[:, None, None, :, None]).reshape(hidden.shape)
        normed = normed * gain_vector + shift_vector
        active = jax.nn.silu(normed).astype(jnp.bfloat16)
        feature_stack = jnp.concatenate([prior_feat, active], axis=0).astype(jnp.float32)
        mixed_sum = convolve(jnp.pad(feature_stack, ((0, 0), (1, 1), (1, 1), (0, 0))), block_full)
        alive_frames = (jnp.arange(frames) < length) & (target >= 0)
        return jnp.where(alive_frames[:, None, None, None], hidden + mixed_sum, 0.0).astype(jnp.bfloat16)
    return lax.map(decode_slab, (latent_slabs, prior_latents, prior_features, lengths, starts, move_plan))
```

```python
import functools

import jax
import jax.numpy as jnp
from jax import lax
from jax.experimental import pallas as pl
from jax.experimental.pallas import tpu as pltpu
from jax.sharding import PartitionSpec as P

GROUPS = 32
EPSILON = 1e-06
LANES = 128


def remote(src, dst, send, recv, axis, target):
    return pltpu.make_async_remote_copy(
        src_ref=src, dst_ref=dst, send_sem=send, recv_sem=recv,
        device_id={axis: target}, device_id_type=pl.DeviceIdType.MESH,
    )


def kernel(
    n_roll, n_rows, cw,
    live_ref, cached_ref, w_ref, pat_ref, feat_ref, we_ref, gain_ref, shift_ref,
    out_ref,
    wg, pg, fg, hid, xc, acc, res, got,
    own_sem, wsend, wrecv, fsend, frecv, psend, precv, gsend, grecv, rsend, rrecv,
):
    me = lax.axis_index("roll")
    row = lax.axis_index("rows")
    sibling = me + 1 - 2 * lax.rem(me, 2)
    half = n_roll // 2
    cwp = w_ref.shape[0]
    width = n_roll * cwp
    slabs, frames, cells, kdim = pat_ref.shape
    feats = gain_ref.shape[1]
    total = n_rows * cells
    chunk = w_ref.shape[1] // 3

    barrier = pltpu.get_barrier_semaphore()
    for s in range(1, n_rows):
        pl.semaphore_signal(barrier, inc=1, device_id={"rows": lax.rem(row + s, n_rows)},
                            device_id_type=pl.DeviceIdType.MESH)
    for s in range(1, half):
        pl.semaphore_signal(barrier, inc=1, device_id={"roll": lax.rem(me + 2 * s, n_roll)},
                            device_id_type=pl.DeviceIdType.MESH)
    pl.semaphore_signal(barrier, inc=1, device_id={"roll": sibling},
                        device_id_type=pl.DeviceIdType.MESH)
    pl.semaphore_wait(barrier, n_rows - 1 + half)

    def piece(ref, a):
        return ref.at[:, pl.ds(a * chunk, chunk)]

    def pat_copy(s):
        return remote(pat_ref, pg.at[row], psend.at[s], precv.at[s], "rows", lax.rem(row + s, n_rows))

    def pat_in(s):
        src = lax.rem(row - s + n_rows, n_rows)
        return remote(pat_ref, pg.at[src], psend.at[s], precv.at[s], "rows", lax.rem(row + s, n_rows))

    def feat_copy(s):
        return remote(feat_ref, fg.at[row], gsend.at[s], grecv.at[s], "rows", lax.rem(row + s, n_rows))

    def direct(s, a):
        return remote(piece(w_ref, a), piece(wg.at[me], a), wsend.at[s, a], wrecv.at[s, a],
                      "roll", lax.rem(me + 2 * s, n_roll))

    def forward(s, a):
        slot = lax.rem(me - 2 * s + n_roll, n_roll)
        src = w_ref if s == 0 else wg.at[slot]
        return remote(piece(src, a), piece(wg.at[slot], a), fsend.at[s, a], frecv.at[s, a],
                      "roll", sibling)

    own = [
        pltpu.make_async_copy(pat_ref, pg.at[row], own_sem.at[0]),
        pltpu.make_async_copy(feat_ref, fg.at[row], own_sem.at[1]),
        pltpu.make_async_copy(w_ref, wg.at[me], own_sem.at[2]),
    ]
    for c in own:
        c.start()
    for s in range(1, n_rows):
        pat_copy(s).start()
    for a in range(3):
        for s in range(1, half):
            direct(s, a).start()
        forward(0, a).start()
    for s in range(1, n_rows):
        feat_copy(s).start()

    own[0].wait()
    for s in range(1, n_rows):
        pat_copy(s).wait_recv()

    lane = lax.broadcasted_iota(jnp.int32, (8, feats), 1)
    sub = lax.broadcasted_iota(jnp.int32, (8, feats), 0)
    column = lax.rem(lax.broadcasted_iota(jnp.int32, (total, feats), 0), 8)
    group = feats // GROUPS
    count = float(total * group)

    def spread(s, f, start, v, col):
        size = v.shape[0]
        rows = pl.ds(start, size)
        xc[s, 1, f, rows, :] = v.astype(jnp.bfloat16)
        xc[s, 0, f, rows, :] = jnp.where(col == 0, 0.0, pltpu.roll(v, 1, 0)).astype(jnp.bfloat16)
        xc[s, 2, f, rows, :] = jnp.where(col == 7, 0.0, pltpu.roll(v, size - 1, 0)).astype(jnp.bfloat16)

    def entry(i, carry):
        s, t = i // frames, lax.rem(i, frames)
        p = jnp.concatenate([pg[z, s, t] for z in range(n_rows)], axis=0)
        ys = [jnp.dot(p, we_ref[b], preferred_element_type=jnp.float32) for b in range(3)]
        zero = jnp.zeros((8, feats), jnp.float32)
        h = (ys[1] + jnp.concatenate([zero, ys[0][:-8]], axis=0)
             + jnp.concatenate([ys[2][8:], zero], axis=0))
        hid[s, t] = h
        first = jnp.sum(h, axis=0, keepdims=True)
        second = jnp.sum(h * h, axis=0, keepdims=True)
        both = jnp.where(sub == 0, first, second)
        k = 1
        while k < group:
            other = jnp.where((lane // k) % 2 == 1, pltpu.roll(both, k, 1),
                              pltpu.roll(both, feats - k, 1))
            both = both + other
            k *= 2
        both = both / count
        mean, square = both[0:1], both[1:2]
        scaled = lax.rsqrt(square - mean * mean + EPSILON)
        v = (h - mean) * scaled * gain_ref[...] + shift_ref[...]
        v = v / (1.0 + jnp.exp(-v))
        spread(s, 2 + t, 0, v, column)
        return carry

    lax.fori_loop(0, slabs * frames // 2, entry, 0)
    for s in range(1, half):
        direct(s, 0).wait_recv()
        forward(s, 0).start()
    lax.fori_loop(slabs * frames // 2, slabs * frames, entry, 0)
    for s in range(1, half):
        direct(s, 1).wait_recv()
        forward(s, 1).start()

    own[1].wait()
    for s in range(1, n_rows):
        feat_copy(s).wait_recv()

    def cache(i, carry):
        s, f = i // 2, lax.rem(i, 2)
        for z in range(n_rows):
            v = fg[z, s, f].astype(jnp.float32)
            v = jnp.where(cached_ref[s] > 0, v, 0.0)
            spread(s, f, z * cells, v, column[:cells])
        return carry

    lax.fori_loop(0, slabs * 2, cache, 0)
    own[2].wait()

    for a in range(3):
        if a == 1:
            for s in range(1, half):
                direct(s, 2).wait_recv()
                forward(s, 2).start()
        for s in range(half):
            forward(s, a).wait_recv()

        def taps(s, carry):
            y = None
            for c in range(3):
                x = xc[s, c, a:a + frames].reshape(frames * total, feats)
                parts = []
                for b in range(3):
                    k0 = ((a * 3 + b) * 3 + c) * feats
                    parts.append(wg[:, :, k0:k0 + feats].reshape(width, feats))
                wmat = jnp.concatenate(parts, axis=0)
                d = lax.dot_general(x, wmat, (((1,), (1,)), ((), ())),
                                    preferred_element_type=jnp.float32)
                y = d if y is None else y + d
            acc[s] = y if a == 0 else acc[s] + y
            return carry

        lax.fori_loop(0, slabs, taps, 0)

    span = n_rows * cw
    tile_lane = lax.broadcasted_iota(jnp.int32, (total, LANES), 1)

    def finish(i, carry):
        s, t = i // frames, lax.rem(i, frames)
        rows = pl.ds(pl.multiple_of(t * total, total), total)
        y = [acc[s, rows, b * width:(b + 1) * width] for b in range(3)]
        zero = jnp.zeros((8, width), jnp.float32)
        m = (y[1] + jnp.concatenate([zero, y[0][:-8]], axis=0)
             + jnp.concatenate([y[2][8:], zero], axis=0))
        tiles = []
        for q in range(width // LANES):
            base = jnp.zeros((total, LANES), jnp.float32)
            for r in range(q * LANES // cwp, (q + 1) * LANES // cwp):
                tile = (r * span) // LANES
                offset = (r * span) % LANES + row * cw
                put = r * cwp - q * LANES
                h = hid[s, t, :, tile * LANES:(tile + 1) * LANES]
                h = pltpu.roll(h, lax.rem(put - offset + 2 * LANES, LANES), 1)
                base = jnp.where((tile_lane >= put) & (tile_lane < put + cw), h, base)
            tiles.append(base)
        hc = jnp.concatenate(tiles, axis=1) if len(tiles) > 1 else tiles[0]
        o = jnp.where(t < live_ref[s], m + hc, 0.0).astype(jnp.bfloat16)
        for z in range(n_rows):
            res[z, s, t] = o[z * cells:(z + 1) * cells]
        return carry

    lax.fori_loop(0, slabs * frames, finish, 0)

    def result(s):
        to = lax.rem(row + s, n_rows)
        return remote(res.at[to], got.at[row], rsend.at[s], rrecv.at[s], "rows", to)

    for s in range(1, n_rows):
        result(s).start()
    got[row] = res[row]
    for s in range(1, n_rows):
        result(s).wait_recv()
    out_ref[...] = got[...]

    for s in range(1, n_rows):
        pat_copy(s).wait_send()
        feat_copy(s).wait_send()
        result(s).wait_send()
    for a in range(3):
        for s in range(1, half):
            direct(s, a).wait_send()
        for s in range(half):
            forward(s, a).wait_send()


def on_device(
    latent_slabs, prior_latents, prior_features, lengths, starts, move_plan,
    entry_weight, block_weight, norm_gain, norm_shift,
):
    n_roll, n_rows = lax.axis_size("roll"), lax.axis_size("rows")
    slabs, frames, height, cols, lat = latent_slabs.shape
    feats = prior_features.shape[-1]
    cells = height * cols
    total = cells * n_rows
    cw = block_weight.shape[1]
    cwp = max(cw, 16)
    width = n_roll * cwp
    kdim = -(-9 * lat // LANES) * LANES
    cached = starts > 0
    prior = jnp.where(cached[:, None, None, None, None], prior_latents, jnp.zeros_like(prior_latents))
    ext = jnp.concatenate([prior, latent_slabs], axis=1)
    ext = jnp.pad(ext, ((0, 0), (0, 0), (0, 0), (1, 1), (0, 0)))
    taps = [ext[:, a:a + frames, :, c:c + cols, :] for a in range(3) for c in range(3)]
    pat = jnp.concatenate(taps, axis=-1)
    pat = jnp.pad(pat, ((0, 0),) * 4 + ((0, kdim - 9 * lat),)).reshape(slabs, frames, cells, kdim)
    we = entry_weight.reshape(3, 3, 3 * lat, feats).transpose(1, 0, 2, 3).reshape(3, 9 * lat, feats)
    we = jnp.pad(we, ((0, 0), (0, kdim - 9 * lat), (0, 0)))
    wt = block_weight.T
    if cwp != cw:
        wt = jnp.pad(wt, ((0, cwp - cw), (0, 0)))
    live = jnp.where(move_plan >= 0, lengths, 0)
    vm = pl.BlockSpec(memory_space=pltpu.VMEM)
    sm = pl.BlockSpec(memory_space=pltpu.SMEM)
    half = n_roll // 2
    dma = pltpu.SemaphoreType.DMA
    out = pl.pallas_call(
        functools.partial(kernel, n_roll, n_rows, cw),
        out_shape=jax.ShapeDtypeStruct((n_rows, slabs, frames, cells, width), jnp.bfloat16),
        in_specs=[sm, sm] + [vm] * 6,
        out_specs=vm,
        scratch_shapes=[
            pltpu.VMEM((n_roll, cwp, wt.shape[1]), jnp.bfloat16),
            pltpu.VMEM((n_rows, slabs, frames, cells, kdim), jnp.bfloat16),
            pltpu.VMEM((n_rows, slabs, 2, cells, feats), jnp.bfloat16),
            pltpu.VMEM((slabs, frames, total, feats), jnp.float32),
            pltpu.VMEM((slabs, 3, frames + 2, total, feats), jnp.bfloat16),
            pltpu.VMEM((slabs, frames * total, 3 * width), jnp.float32),
            pltpu.VMEM((n_rows, slabs, frames, cells, width), jnp.bfloat16),
            pltpu.VMEM((n_rows, slabs, frames, cells, width), jnp.bfloat16),
            dma((3,)),
            dma((half, 3)), dma((half, 3)), dma((half, 3)), dma((half, 3)),
            dma((n_rows,)), dma((n_rows,)), dma((n_rows,)), dma((n_rows,)),
            dma((n_rows,)), dma((n_rows,)),
        ],
        compiler_params=pltpu.CompilerParams(
            collective_id=0, has_side_effects=True, vmem_limit_bytes=67043328
        ),
        name="decode",
    )(
        live, cached.astype(jnp.int32), wt, pat,
        prior_features.reshape(slabs, 2, cells, feats), we,
        norm_gain[None], norm_shift[None],
    )
    out = out.reshape(n_rows, slabs, frames, cells, n_roll, cwp)[..., :cw]
    out = out.transpose(1, 2, 3, 4, 0, 5)
    return out.reshape(slabs, frames, height, cols, feats)


def solution(mesh):
    in_specs = (
        P(("groups", "roll"), None, "rows", None, None),
        P(("groups", "roll"), None, "rows", None, None),
        P(("groups", "roll"), None, "rows", None, None),
        P(("groups", "roll")),
        P(("groups", "roll")),
        P(("groups", "roll")),
        P(),
        P(None, ("roll", "rows")),
        P(),
        P(),
    )
    out_specs = P(("groups", "roll"), None, "rows", None, None)
    return jax.shard_map(
        on_device, mesh=mesh, in_specs=in_specs, out_specs=out_specs, check_vma=False
    )
```

```python
import functools

import jax
import jax.numpy as jnp
from jax import lax
from jax.experimental import pallas as pl
from jax.experimental.pallas import tpu as pltpu
from jax.sharding import PartitionSpec as P

GROUPS = 32
EPSILON = 1e-06
LANES = 128


def remote(src, dst, send, recv, axis, target):
    return pltpu.make_async_remote_copy(
        src_ref=src, dst_ref=dst, send_sem=send, recv_sem=recv,
        device_id={axis: target}, device_id_type=pl.DeviceIdType.MESH,
    )


def kernel(
    n_roll, n_rows, cw,
    lengths_ref, starts_ref, plan_ref, w_ref, lat_ref, feat_ref, ew_ref, gain_ref, shift_ref,
    out_ref,
    wg, lg, fg, wes, xs, hid, xc, acc, res, got,
    own_sem, wsend, wrecv, fsend, frecv, lsend, lrecv, gsend, grecv, rsend, rrecv,
):
    me = lax.axis_index("roll")
    row = lax.axis_index("rows")
    sibling = me + 1 - 2 * lax.rem(me, 2)
    half = n_roll // 2
    cwp = w_ref.shape[0]
    width = n_roll * cwp
    slabs, depth, height, dense = lat_ref.shape
    frames = depth - 2
    cols = feat_ref.shape[3]
    lat = dense // cols
    cells = height * cols
    feats = gain_ref.shape[1]
    total = n_rows * cells
    chunk = w_ref.shape[1] // 3

    barrier = pltpu.get_barrier_semaphore()
    for s in range(1, n_rows):
        pl.semaphore_signal(barrier, inc=1, device_id={"rows": lax.rem(row + s, n_rows)},
                            device_id_type=pl.DeviceIdType.MESH)
    for s in range(1, half):
        pl.semaphore_signal(barrier, inc=1, device_id={"roll": lax.rem(me + 2 * s, n_roll)},
                            device_id_type=pl.DeviceIdType.MESH)
    pl.semaphore_signal(barrier, inc=1, device_id={"roll": sibling},
                        device_id_type=pl.DeviceIdType.MESH)
    wes[...] = jnp.zeros_like(wes)
    for a in range(3):
        for b in range(3):
            k0 = (a * 3 + b) * 3 * lat
            wes[b, a * dense // 2:a * dense // 2 + 3 * lat] = ew_ref[k0:k0 + 3 * lat]
    pl.semaphore_wait(barrier, n_rows - 1 + half)

    def piece(ref, a):
        return ref.at[:, pl.ds(a * chunk, chunk)]

    def lat_copy(s):
        return remote(lat_ref, lg.at[row], lsend.at[s], lrecv.at[s], "rows", lax.rem(row + s, n_rows))

    def hop(k, way):
        src = lax.rem(row - way * k + n_rows, n_rows)
        to = lax.rem(row + way + n_rows, n_rows)
        d = 0 if way > 0 else 1
        return remote(feat_ref if k == 0 else fg.at[src], fg.at[src],
                      gsend.at[d, k], grecv.at[d, k], "rows", to)

    def sends(k, way):
        if way > 0:
            return (row >= k) & (row < n_rows - 1)
        return (row + k < n_rows) & (row > 0)

    def receives(k, way):
        return row > k if way > 0 else row + k + 1 < n_rows

    def relay(k):
        for way in (1, -1):
            if k > 0:
                @pl.when(receives(k - 1, way))
                def _():
                    hop(k - 1, way).wait_recv()
            if k < n_rows - 1:
                @pl.when(sends(k, way))
                def _():
                    hop(k, way).start()

    def direct(s, a):
        return remote(piece(w_ref, a), piece(wg.at[me], a), wsend.at[s, a], wrecv.at[s, a],
                      "roll", lax.rem(me + 2 * s, n_roll))

    def forward(s, a):
        slot = lax.rem(me - 2 * s + n_roll, n_roll)
        src = w_ref if s == 0 else wg.at[slot]
        return remote(piece(src, a), piece(wg.at[slot], a), fsend.at[s, a], frecv.at[s, a],
                      "roll", sibling)

    own = [
        pltpu.make_async_copy(lat_ref, lg.at[row], own_sem.at[0]),
        pltpu.make_async_copy(feat_ref, fg.at[row], own_sem.at[1]),
        pltpu.make_async_copy(w_ref, wg.at[me], own_sem.at[2]),
    ]
    for c in own:
        c.start()
    for s in range(1, n_rows):
        lat_copy(s).start()
    relay(0)
    order = (2, 1, 0)
    for a in order:
        for s in range(1, half):
            direct(s, a).start()
        forward(0, a).start()

    def pass_on(a):
        for s in range(1, half):
            direct(s, a).wait_recv()
            forward(s, a).start()

    own[0].wait()
    for s in range(1, n_rows):
        lat_copy(s).wait_recv()

    lane = lax.broadcasted_iota(jnp.int32, (8, feats), 1)
    sub = lax.broadcasted_iota(jnp.int32, (8, feats), 0)
    column = lax.rem(lax.broadcasted_iota(jnp.int32, (total, feats), 0), cols)
    group = feats // GROUPS
    count = float(total * group)
    high = n_rows * height
    at = lax.broadcasted_iota(jnp.int32, (high, cols, dense), 1)
    place = lax.broadcasted_iota(jnp.int32, (high, cols, dense), 2)
    keep = (place < 3 * lat) & ((at > 0) | (place >= lat)) & ((at < cols - 1) | (place < 2 * lat))

    def expand(i, carry):
        s, f = i // depth, lax.rem(i, depth)
        r = jnp.concatenate([lg[z, s, f].astype(jnp.float32) for z in range(n_rows)], axis=0)
        x = jnp.zeros((high, cols, dense), jnp.float32)
        for j in range(cols):
            move = (dense - lat * (j - 1)) % dense
            rj = pltpu.roll(r, move, 1) if move else r
            x = jnp.where(at == j, rj[:, None, :], x)
        x = jnp.where(keep & ((f >= 2) | (starts_ref[s] > 0)), x, 0.0)
        xs[s, f] = x.reshape(total, dense)
        return carry

    lax.fori_loop(0, slabs * depth, expand, 0)

    def spread(s, f, start, v, col):
        size = v.shape[0]
        rows = pl.ds(start, size)
        xc[s, 1, f, rows, :] = v.astype(jnp.bfloat16)
        xc[s, 0, f, rows, :] = jnp.where(col == 0, 0.0, pltpu.roll(v, 1, 0)).astype(jnp.bfloat16)
        xc[s, 2, f, rows, :] = jnp.where(
            col == cols - 1, 0.0, pltpu.roll(v, size - 1, 0)).astype(jnp.bfloat16)

    def entry(i, carry):
        s, t = i // frames, lax.rem(i, frames)
        p = jnp.concatenate(
            [xs[s, t] + pltpu.roll(xs[s, t + 1], dense // 2, 1), xs[s, t + 2]], axis=1
        ).astype(jnp.bfloat16)
        ys = [jnp.dot(p, wes[b], preferred_element_type=jnp.float32) for b in range(3)]
        zero = jnp.zeros((cols, feats), jnp.float32)
        h = (ys[1] + jnp.concatenate([zero, ys[0][:-cols]], axis=0)
             + jnp.concatenate([ys[2][cols:], zero], axis=0))
        hid[s, t] = h
        first = jnp.sum(h, axis=0, keepdims=True)
        second = jnp.sum(h * h, axis=0, keepdims=True)
        both = jnp.where(sub == 0, first, second)
        k = 1
        while k < group:
            other = jnp.where((lane // k) % 2 == 1, pltpu.roll(both, k, 1),
                              pltpu.roll(both, feats - k, 1))
            both = both + other
            k *= 2
        both = both / count
        mean, square = both[0:1], both[1:2]
        scaled = lax.rsqrt(square - mean * mean + EPSILON)
        v = (h - mean) * scaled * gain_ref[...] + shift_ref[...]
        v = v / (1.0 + jnp.exp(-v))
        spread(s, 2 + t, 0, v, column)
        return carry

    lax.fori_loop(0, slabs * frames // 2, entry, 0)
    relay(1)
    pass_on(order[0])
    lax.fori_loop(slabs * frames // 2, slabs * frames, entry, 0)
    relay(2)
    pass_on(order[1])
    own[2].wait()

    def arrive(a):
        for s in range(half):
            forward(s, a).wait_recv()

    def taps(a, s):
        y = None
        for c in range(3):
            x = xc[s, c, a:a + frames].reshape(frames * total, feats)
            parts = []
            for b in range(3):
                k0 = ((a * 3 + b) * 3 + c) * feats
                parts.append(wg[:, :, k0:k0 + feats].reshape(width, feats))
            wmat = jnp.concatenate(parts, axis=0)
            d = lax.dot_general(x, wmat, (((1,), (1,)), ((), ())),
                                preferred_element_type=jnp.float32)
            y = d if y is None else y + d
        acc[s] = y if a == order[0] else acc[s] + y

    def each(a):
        def body(s, carry):
            taps(a, s)
            return carry
        lax.fori_loop(0, slabs, body, 0)

    arrive(order[0])
    each(order[0])

    for k in range(3, n_rows):
        relay(k)
    own[1].wait()

    def cache(i, carry):
        s, f = i // 2, lax.rem(i, 2)
        for z in range(n_rows):
            v = fg[z, s, f].astype(jnp.float32).reshape(cells, feats)
            v = jnp.where(starts_ref[s] > 0, v, 0.0)
            spread(s, f, z * cells, v, column[:cells])
        return carry

    lax.fori_loop(0, slabs * 2, cache, 0)
    pass_on(order[2])
    arrive(order[1])
    each(order[1])
    arrive(order[2])

    span = n_rows * cw
    tile_lane = lax.broadcasted_iota(jnp.int32, (total, LANES), 1)

    def finish(s, t):
        rows = pl.ds(pl.multiple_of(t * total, total), total)
        y = [acc[s, rows, b * width:(b + 1) * width] for b in range(3)]
        zero = jnp.zeros((cols, width), jnp.float32)
        m = (y[1] + jnp.concatenate([zero, y[0][:-cols]], axis=0)
             + jnp.concatenate([y[2][cols:], zero], axis=0))
        tiles = []
        for q in range(width // LANES):
            base = jnp.zeros((total, LANES), jnp.float32)
            for r in range(q * LANES // cwp, (q + 1) * LANES // cwp):
                tile = (r * span) // LANES
                offset = (r * span) % LANES + row * cw
                put = r * cwp - q * LANES
                h = hid[s, t, :, tile * LANES:(tile + 1) * LANES]
                h = pltpu.roll(h, lax.rem(put - offset + 2 * LANES, LANES), 1)
                base = jnp.where((tile_lane >= put) & (tile_lane < put + cw), h, base)
            tiles.append(base)
        hc = jnp.concatenate(tiles, axis=1) if len(tiles) > 1 else tiles[0]
        live = (plan_ref[s] >= 0) & (t < lengths_ref[s])
        o = jnp.where(live, m + hc, 0.0).astype(jnp.bfloat16)
        for z in range(n_rows):
            res[s, z, t] = o[z * cells:(z + 1) * cells]

    def result(s, k):
        to = lax.rem(row + k, n_rows)
        return remote(res.at[s, to], got.at[s, row], rsend.at[s, k], rrecv.at[s, k], "rows", to)

    for s in range(slabs):
        taps(order[2], s)

        def close(t, carry, s=s):
            finish(s, t)
            return carry

        lax.fori_loop(0, frames, close, 0)
        for k in range(1, n_rows):
            result(s, k).start()
        got[s, row] = res[s, row]

    owner_lane = lax.broadcasted_iota(jnp.int32, (cells, LANES), 1)
    for s in range(slabs):
        for k in range(1, n_rows):
            result(s, k).wait_recv()

        def gather(t, carry, s=s):
            tiles = [jnp.zeros((cells, LANES), jnp.float32) for _ in range(feats // LANES)]
            for z in range(n_rows):
                g = got[s, z, t].astype(jnp.float32)
                for r in range(n_roll):
                    q, take = (r * cwp) // LANES, (r * cwp) % LANES
                    start = (r * n_rows + z) * cw
                    tile, put = start // LANES, start % LANES
                    h = g[:, q * LANES:(q + 1) * LANES]
                    move = (put - take) % LANES
                    if move:
                        h = pltpu.roll(h, move, 1)
                    tiles[tile] = jnp.where(
                        (owner_lane >= put) & (owner_lane < put + cw), h, tiles[tile])
            o = jnp.concatenate(tiles, axis=1)
            out_ref[s, t] = o.reshape(height, cols, feats).astype(jnp.bfloat16)
            return carry

        lax.fori_loop(0, frames, gather, 0)

    for s in range(1, n_rows):
        lat_copy(s).wait_send()
        for i in range(slabs):
            result(i, s).wait_send()
    for k in range(n_rows - 1):
        for way in (1, -1):
            @pl.when(sends(k, way))
            def _():
                hop(k, way).wait_send()
    for a in range(3):
        for s in range(1, half):
            direct(s, a).wait_send()
        for s in range(half):
            forward(s, a).wait_send()


def on_device(
    latent_slabs, prior_latents, prior_features, lengths, starts, move_plan,
    entry_weight, block_weight, norm_gain, norm_shift,
):
    n_roll, n_rows = lax.axis_size("roll"), lax.axis_size("rows")
    slabs, frames, height, cols, lat = latent_slabs.shape
    feats = prior_features.shape[-1]
    cells = height * cols
    total = cells * n_rows
    dense = cols * lat
    cw = block_weight.shape[1]
    cwp = max(cw, 16)
    width = n_roll * cwp
    dense_lat = jnp.concatenate([prior_latents, latent_slabs], axis=1).reshape(
        slabs, frames + 2, height, dense)
    wt = block_weight.T
    if cwp != cw:
        wt = jnp.pad(wt, ((0, cwp - cw), (0, 0)))
    vm = pl.BlockSpec(memory_space=pltpu.VMEM)
    sm = pl.BlockSpec(memory_space=pltpu.SMEM)
    half = n_roll // 2
    dma = pltpu.SemaphoreType.DMA
    return pl.pallas_call(
        functools.partial(kernel, n_roll, n_rows, cw),
        out_shape=jax.ShapeDtypeStruct((slabs, frames, height, cols, feats), jnp.bfloat16),
        in_specs=[sm] * 3 + [vm] * 6,
        out_specs=vm,
        scratch_shapes=[
            pltpu.VMEM((n_roll, cwp, wt.shape[1]), jnp.bfloat16),
            pltpu.VMEM((n_rows, slabs, frames + 2, height, dense), jnp.bfloat16),
            pltpu.VMEM((n_rows, slabs, 2, height, cols, feats), jnp.bfloat16),
            pltpu.VMEM((3, 2 * dense, feats), jnp.bfloat16),
            pltpu.VMEM((slabs, frames + 2, total, dense), jnp.float32),
            pltpu.VMEM((slabs, frames, total, feats), jnp.float32),
            pltpu.VMEM((slabs, 3, frames + 2, total, feats), jnp.bfloat16),
            pltpu.VMEM((slabs, frames * total, 3 * width), jnp.float32),
            pltpu.VMEM((slabs, n_rows, frames, cells, width), jnp.bfloat16),
            pltpu.VMEM((slabs, n_rows, frames, cells, width), jnp.bfloat16),
            dma((3,)),
            dma((half, 3)), dma((half, 3)), dma((half, 3)), dma((half, 3)),
            dma((n_rows,)), dma((n_rows,)),
            dma((2, n_rows)), dma((2, n_rows)),
            dma((slabs, n_rows)), dma((slabs, n_rows)),
        ],
        compiler_params=pltpu.CompilerParams(
            collective_id=0, has_side_effects=True, vmem_limit_bytes=67043328
        ),
        name="decode",
    )(
        lengths, starts, move_plan, wt, dense_lat, prior_features, entry_weight,
        norm_gain[None], norm_shift[None],
    )


def solution(mesh):
    in_specs = (
        P(("groups", "roll"), None, "rows", None, None),
        P(("groups", "roll"), None, "rows", None, None),
        P(("groups", "roll"), None, "rows", None, None),
        P(("groups", "roll")),
        P(("groups", "roll")),
        P(("groups", "roll")),
        P(),
        P(None, ("roll", "rows")),
        P(),
        P(),
    )
    out_specs = P(("groups", "roll"), None, "rows", None, None)
    return jax.shard_map(
        on_device, mesh=mesh, in_specs=in_specs, out_specs=out_specs, check_vma=False
    )
```

```python
import functools

import jax
import jax.numpy as jnp
from jax import lax
from jax.experimental import pallas as pl
from jax.experimental.pallas import tpu as pltpu
from jax.sharding import PartitionSpec as P

GROUPS = 32
EPSILON = 1e-06
LANES = 128


def remote(src, dst, send, recv, axis, target):
    return pltpu.make_async_remote_copy(
        src_ref=src, dst_ref=dst, send_sem=send, recv_sem=recv,
        device_id={axis: target}, device_id_type=pl.DeviceIdType.MESH,
    )


def kernel(
    n_groups, n_roll, n_rows, cw,
    lengths_ref, starts_ref, plan_ref, w_ref, lat_ref, feat_ref, ew_ref, gain_ref, shift_ref,
    out_ref,
    wg, lg, fg, wes, xs, hid, xc, acc, res, got,
    own_sem, wsend, wrecv, xsend, xrecv, fsend, frecv, lsend, lrecv, gsend, grecv, rsend, rrecv,
):
    me = lax.axis_index("roll")
    row = lax.axis_index("rows")
    mine = lax.axis_index("groups") if n_groups == 2 else 0
    sibling = me + 1 - 2 * lax.rem(me, 2)
    half = n_roll // 2
    cwp = w_ref.shape[0]
    width = n_roll * cwp
    slabs, depth, height, dense = lat_ref.shape
    frames = depth - 2
    cols = feat_ref.shape[3]
    lat = dense // cols
    cells = height * cols
    feats = gain_ref.shape[1]
    total = n_rows * cells
    chunk = w_ref.shape[1] // 3
    part = chunk // n_groups if n_groups == 2 else chunk

    barrier = pltpu.get_barrier_semaphore()
    for s in range(1, n_rows):
        pl.semaphore_signal(barrier, inc=1, device_id={"rows": lax.rem(row + s, n_rows)},
                            device_id_type=pl.DeviceIdType.MESH)
    for s in range(1, half):
        pl.semaphore_signal(barrier, inc=1, device_id={"roll": lax.rem(me + 2 * s, n_roll)},
                            device_id_type=pl.DeviceIdType.MESH)
    pl.semaphore_signal(barrier, inc=1, device_id={"roll": sibling},
                        device_id_type=pl.DeviceIdType.MESH)
    if n_groups == 2:
        pl.semaphore_signal(barrier, inc=1, device_id={"groups": 1 - mine},
                            device_id_type=pl.DeviceIdType.MESH)
    wes[...] = jnp.zeros_like(wes)
    for a in range(3):
        for b in range(3):
            k0 = (a * 3 + b) * 3 * lat
            wes[b, a * dense // 2:a * dense // 2 + 3 * lat] = ew_ref[k0:k0 + 3 * lat]
    pl.semaphore_wait(barrier, n_rows - 1 + half + (n_groups == 2))

    def piece(ref, a):
        return ref.at[:, pl.ds(a * chunk, chunk)]

    def lat_copy(s):
        return remote(lat_ref, lg.at[row], lsend.at[s], lrecv.at[s], "rows", lax.rem(row + s, n_rows))

    def hop(k, way):
        src = lax.rem(row - way * k + n_rows, n_rows)
        to = lax.rem(row + way + n_rows, n_rows)
        d = 0 if way > 0 else 1
        return remote(feat_ref if k == 0 else fg.at[src], fg.at[src],
                      gsend.at[d, k], grecv.at[d, k], "rows", to)

    def sends(k, way):
        if way > 0:
            return (row >= k) & (row < n_rows - 1)
        return (row + k < n_rows) & (row > 0)

    def receives(k, way):
        return row > k if way > 0 else row + k + 1 < n_rows

    def relay(k):
        for way in (1, -1):
            if k > 0:
                @pl.when(receives(k - 1, way))
                def _():
                    hop(k - 1, way).wait_recv()
            if k < n_rows - 1:
                @pl.when(sends(k, way))
                def _():
                    hop(k, way).start()

    def share(ref, a, h):
        return ref.at[:, pl.ds(pl.multiple_of(a * chunk + h * part, LANES), part)]

    def direct(s, a):
        return remote(share(w_ref, a, mine), share(wg.at[me], a, mine), wsend.at[s, a],
                      wrecv.at[s, a], "roll", lax.rem(me + 2 * s, n_roll))

    def slot_of(s):
        return lax.rem(me - 2 * s + n_roll, n_roll)

    def swap(s, a):
        block = share(wg.at[slot_of(s)], a, mine)
        return remote(block, block, xsend.at[s, a], xrecv.at[s, a], "groups", 1 - mine)

    def give(a):
        return remote(piece(w_ref, a), piece(wg.at[me], a), fsend.at[0, 0, a], frecv.at[0, 0, a],
                      "roll", sibling)

    def forward(s, a, u):
        block = share(wg.at[slot_of(s)], a, mine if u == 0 else 1 - mine)
        return remote(block, block, fsend.at[u, s, a], frecv.at[u, s, a], "roll", sibling)

    own = [
        pltpu.make_async_copy(lat_ref, lg.at[row], own_sem.at[0]),
        pltpu.make_async_copy(feat_ref, fg.at[row], own_sem.at[1]),
        pltpu.make_async_copy(w_ref, wg.at[me], own_sem.at[2]),
    ]
    for c in own:
        c.start()
    for s in range(1, n_rows):
        lat_copy(s).start()
    relay(0)
    for a in (2, 1, 0):
        for s in range(1, half):
            direct(s, a).start()
        give(a).start()

    def pass_on(a):
        for s in range(1, half):
            direct(s, a).wait_recv()
            if n_groups == 2:
                swap(s, a).start()
            forward(s, a, 0).start()

    def pass_swap(a):
        if n_groups == 2:
            for s in range(1, half):
                swap(s, a).wait_recv()
                forward(s, a, 1).start()

    own[0].wait()
    for s in range(1, n_rows):
        lat_copy(s).wait_recv()

    lane = lax.broadcasted_iota(jnp.int32, (8, feats), 1)
    sub = lax.broadcasted_iota(jnp.int32, (8, feats), 0)
    column = lax.rem(lax.broadcasted_iota(jnp.int32, (total, feats), 0), cols)
    group = feats // GROUPS
    count = float(total * group)
    high = n_rows * height
    at = lax.broadcasted_iota(jnp.int32, (high, cols, dense), 1)
    place = lax.broadcasted_iota(jnp.int32, (high, cols, dense), 2)
    keep = (place < 3 * lat) & ((at > 0) | (place >= lat)) & ((at < cols - 1) | (place < 2 * lat))

    def expand(i, carry):
        s, f = i // depth, lax.rem(i, depth)
        r = jnp.concatenate([lg[z, s, f].astype(jnp.float32) for z in range(n_rows)], axis=0)
        x = jnp.zeros((high, cols, dense), jnp.float32)
        for j in range(cols):
            move = (dense - lat * (j - 1)) % dense
            rj = pltpu.roll(r, move, 1) if move else r
            x = jnp.where(at == j, rj[:, None, :], x)
        x = jnp.where(keep & ((f >= 2) | (starts_ref[s] > 0)), x, 0.0)
        xs[s, f] = x.reshape(total, dense)
        return carry

    lax.fori_loop(0, slabs * depth, expand, 0)

    def spread(s, f, start, v, col):
        size = v.shape[0]
        rows = pl.ds(start, size)
        xc[s, 1, f, rows, :] = v.astype(jnp.bfloat16)
        xc[s, 0, f, rows, :] = jnp.where(col == 0, 0.0, pltpu.roll(v, 1, 0)).astype(jnp.bfloat16)
        xc[s, 2, f, rows, :] = jnp.where(
            col == cols - 1, 0.0, pltpu.roll(v, size - 1, 0)).astype(jnp.bfloat16)

    def entry(i, carry):
        s, t = i // frames, lax.rem(i, frames)
        p = jnp.concatenate(
            [xs[s, t] + pltpu.roll(xs[s, t + 1], dense // 2, 1), xs[s, t + 2]], axis=1
        ).astype(jnp.bfloat16)
        ys = [jnp.dot(p, wes[b], preferred_element_type=jnp.float32) for b in range(3)]
        zero = jnp.zeros((cols, feats), jnp.float32)
        h = (ys[1] + jnp.concatenate([zero, ys[0][:-cols]], axis=0)
             + jnp.concatenate([ys[2][cols:], zero], axis=0))
        hid[s, t] = h
        first = jnp.sum(h, axis=0, keepdims=True)
        second = jnp.sum(h * h, axis=0, keepdims=True)
        both = jnp.where(sub == 0, first, second)
        k = 1
        while k < group:
            other = jnp.where((lane // k) % 2 == 1, pltpu.roll(both, k, 1),
                              pltpu.roll(both, feats - k, 1))
            both = both + other
            k *= 2
        both = both / count
        mean, square = both[0:1], both[1:2]
        scaled = lax.rsqrt(square - mean * mean + EPSILON)
        v = (h - mean) * scaled * gain_ref[...] + shift_ref[...]
        v = v / (1.0 + jnp.exp(-v))
        spread(s, 2 + t, 0, v, column)
        return carry

    jobs = slabs * frames
    lax.fori_loop(0, jobs // 3, entry, 0)
    pass_on(2)
    lax.fori_loop(jobs // 3, 2 * jobs // 3, entry, 0)
    pass_on(1)
    relay(1)
    pass_swap(2)
    lax.fori_loop(2 * jobs // 3, jobs, entry, 0)
    pass_on(0)
    pass_swap(1)
    own[2].wait()

    def arrive(a):
        give(a).wait_recv()
        for s in range(1, half):
            forward(s, a, 0).wait_recv()
            if n_groups == 2:
                forward(s, a, 1).wait_recv()

    def taps(a, s, t0, t1):
        y = None
        for c in range(3):
            x = xc[s, c, a + t0:a + t1].reshape((t1 - t0) * total, feats)
            parts = []
            for b in range(3):
                k0 = ((a * 3 + b) * 3 + c) * feats
                parts.append(wg[:, :, k0:k0 + feats].reshape(width, feats))
            wmat = jnp.concatenate(parts, axis=0)
            d = lax.dot_general(x, wmat, (((1,), (1,)), ((), ())),
                                preferred_element_type=jnp.float32)
            y = d if y is None else y + d
        rows = slice(t0 * total, t1 * total)
        acc[s, rows] = y if a == 2 else acc[s, rows] + y

    def each(a, t0, t1):
        def body(s, carry):
            taps(a, s, t0, t1)
            return carry
        lax.fori_loop(0, slabs, body, 0)

    arrive(2)
    each(2, 0, frames)
    relay(2)
    pass_swap(0)
    arrive(1)
    each(1, 1, frames)
    arrive(0)

    span = n_rows * cw
    tile_lane = lax.broadcasted_iota(jnp.int32, (total, LANES), 1)

    def finish(s, t):
        rows = pl.ds(t * total, total)
        y = [acc[s, rows, b * width:(b + 1) * width] for b in range(3)]
        zero = jnp.zeros((cols, width), jnp.float32)
        m = (y[1] + jnp.concatenate([zero, y[0][:-cols]], axis=0)
             + jnp.concatenate([y[2][cols:], zero], axis=0))
        tiles = []
        for q in range(width // LANES):
            base = jnp.zeros((total, LANES), jnp.float32)
            for r in range(q * LANES // cwp, (q + 1) * LANES // cwp):
                tile = (r * span) // LANES
                offset = (r * span) % LANES + row * cw
                put = r * cwp - q * LANES
                h = hid[s, t, :, tile * LANES:(tile + 1) * LANES]
                h = pltpu.roll(h, lax.rem(put - offset + 2 * LANES, LANES), 1)
                base = jnp.where((tile_lane >= put) & (tile_lane < put + cw), h, base)
            tiles.append(base)
        hc = jnp.concatenate(tiles, axis=1) if len(tiles) > 1 else tiles[0]
        live = (plan_ref[s] >= 0) & (t < lengths_ref[s])
        o = jnp.where(live, m + hc, 0.0).astype(jnp.bfloat16)
        for z in range(n_rows):
            res[s, z, t] = o[z * cells:(z + 1) * cells]

    def late(u):
        return pl.ds(2, frames - 2) if u == 0 else pl.ds(0, 2)

    def result(s, u, k):
        to = lax.rem(row + k, n_rows)
        return remote(res.at[s, to, late(u)], got.at[s, row, late(u)],
                      rsend.at[s, u, k], rrecv.at[s, u, k], "rows", to)

    def close(s, u):
        for t in range(2, frames) if u == 0 else range(2):
            finish(s, t)
        for k in range(1, n_rows):
            result(s, u, k).start()
        got[s, row, late(u)] = res[s, row, late(u)]

    for s in range(slabs):
        taps(0, s, 2, frames)
        close(s, 0)

    for k in range(3, n_rows):
        relay(k)
    own[1].wait()

    def cache(i, carry):
        s, f = i // 2, lax.rem(i, 2)
        for z in range(n_rows):
            v = fg[z, s, f].astype(jnp.float32).reshape(cells, feats)
            v = jnp.where(starts_ref[s] > 0, v, 0.0)
            spread(s, f, z * cells, v, column[:cells])
        return carry

    lax.fori_loop(0, slabs * 2, cache, 0)
    for s in range(slabs):
        taps(1, s, 0, 1)
        taps(0, s, 0, 2)
        close(s, 1)

    owner_lane = lax.broadcasted_iota(jnp.int32, (cells, LANES), 1)

    def placed(s, t):
        tiles = [jnp.zeros((cells, LANES), jnp.float32) for _ in range(feats // LANES)]
        for z in range(n_rows):
            g = got[s, z, t].astype(jnp.float32)
            for r in range(n_roll):
                q, take = (r * cwp) // LANES, (r * cwp) % LANES
                start = (r * n_rows + z) * cw
                tile, put = start // LANES, start % LANES
                h = g[:, q * LANES:(q + 1) * LANES]
                move = (put - take) % LANES
                if move:
                    h = pltpu.roll(h, move, 1)
                tiles[tile] = jnp.where(
                    (owner_lane >= put) & (owner_lane < put + cw), h, tiles[tile])
        o = jnp.concatenate(tiles, axis=1)
        out_ref[s, t] = o.reshape(height, cols, feats).astype(jnp.bfloat16)

    for u in range(2):
        for s in range(slabs):
            for k in range(1, n_rows):
                result(s, u, k).wait_recv()

            def gather(t, carry, s=s):
                placed(s, t)
                return carry

            lax.fori_loop(2 if u == 0 else 0, frames if u == 0 else 2, gather, 0)

    for s in range(1, n_rows):
        lat_copy(s).wait_send()
        for i in range(slabs):
            for u in range(2):
                result(i, u, s).wait_send()
    for k in range(n_rows - 1):
        for way in (1, -1):
            @pl.when(sends(k, way))
            def _():
                hop(k, way).wait_send()
    for a in range(3):
        give(a).wait_send()
        for s in range(1, half):
            direct(s, a).wait_send()
            forward(s, a, 0).wait_send()
            if n_groups == 2:
                swap(s, a).wait_send()
                forward(s, a, 1).wait_send()


def on_device(
    latent_slabs, prior_latents, prior_features, lengths, starts, move_plan,
    entry_weight, block_weight, norm_gain, norm_shift,
):
    n_roll, n_rows = lax.axis_size("roll"), lax.axis_size("rows")
    slabs, frames, height, cols, lat = latent_slabs.shape
    feats = prior_features.shape[-1]
    cells = height * cols
    total = cells * n_rows
    dense = cols * lat
    cw = block_weight.shape[1]
    cwp = max(cw, 16)
    width = n_roll * cwp
    dense_lat = jnp.concatenate([prior_latents, latent_slabs], axis=1).reshape(
        slabs, frames + 2, height, dense)
    wt = block_weight.T
    if cwp != cw:
        wt = jnp.pad(wt, ((0, cwp - cw), (0, 0)))
    vm = pl.BlockSpec(memory_space=pltpu.VMEM)
    sm = pl.BlockSpec(memory_space=pltpu.SMEM)
    hbm = pl.BlockSpec(memory_space=pl.ANY)
    half = n_roll // 2
    dma = pltpu.SemaphoreType.DMA
    return pl.pallas_call(
        functools.partial(kernel, lax.axis_size("groups"), n_roll, n_rows, cw),
        out_shape=jax.ShapeDtypeStruct((slabs, frames, height, cols, feats), jnp.bfloat16),
        in_specs=[sm] * 3 + [hbm, vm, hbm] + [vm] * 3,
        out_specs=vm,
        scratch_shapes=[
            pltpu.VMEM((n_roll, cwp, wt.shape[1]), jnp.bfloat16),
            pltpu.VMEM((n_rows, slabs, frames + 2, height, dense), jnp.bfloat16),
            pltpu.VMEM((n_rows, slabs, 2, height, cols, feats), jnp.bfloat16),
            pltpu.VMEM((3, 2 * dense, feats), jnp.bfloat16),
            pltpu.VMEM((slabs, frames + 2, total, dense), jnp.float32),
            pltpu.VMEM((slabs, frames, total, feats), jnp.float32),
            pltpu.VMEM((slabs, 3, frames + 2, total, feats), jnp.bfloat16),
            pltpu.VMEM((slabs, frames * total, 3 * width), jnp.float32),
            pltpu.VMEM((slabs, n_rows, frames, cells, width), jnp.bfloat16),
            pltpu.VMEM((slabs, n_rows, frames, cells, width), jnp.bfloat16),
            dma((3,)),
            dma((half, 3)), dma((half, 3)), dma((half, 3)), dma((half, 3)),
            dma((2, half, 3)), dma((2, half, 3)),
            dma((n_rows,)), dma((n_rows,)),
            dma((2, n_rows)), dma((2, n_rows)),
            dma((slabs, 2, n_rows)), dma((slabs, 2, n_rows)),
        ],
        compiler_params=pltpu.CompilerParams(
            collective_id=0, has_side_effects=True, vmem_limit_bytes=67043328
        ),
        name="decode",
    )(
        lengths, starts, move_plan, wt, dense_lat, prior_features, entry_weight,
        norm_gain[None], norm_shift[None],
    )


def solution(mesh):
    in_specs = (
        P(("groups", "roll"), None, "rows", None, None),
        P(("groups", "roll"), None, "rows", None, None),
        P(("groups", "roll"), None, "rows", None, None),
        P(("groups", "roll")),
        P(("groups", "roll")),
        P(("groups", "roll")),
        P(),
        P(None, ("roll", "rows")),
        P(),
        P(),
    )
    out_specs = P(("groups", "roll"), None, "rows", None, None)
    return jax.shard_map(
        on_device, mesh=mesh, in_specs=in_specs, out_specs=out_specs, check_vma=False
    )
```

```python
import functools

import jax
import jax.numpy as jnp
from jax import lax
from jax.experimental import pallas as pl
from jax.experimental.pallas import tpu as pltpu
from jax.sharding import PartitionSpec as P

GROUPS = 32
EPSILON = 1e-06
LANES = 128


def remote(src, dst, send, recv, axis, target):
    return pltpu.make_async_remote_copy(
        src_ref=src, dst_ref=dst, send_sem=send, recv_sem=recv,
        device_id={axis: target}, device_id_type=pl.DeviceIdType.MESH,
    )


def kernel(
    n_groups, n_roll, n_rows, cw,
    lengths_ref, starts_ref, plan_ref, w_ref, lat_ref, feat_ref, ew_ref, gain_ref, shift_ref,
    out_ref,
    wg, lg, fg, wes, xs, hid, xc, acc, res, got,
    own_sem, wsend, wrecv, xsend, xrecv, fsend, frecv, lsend, lrecv, gsend, grecv, rsend, rrecv,
):
    me = lax.axis_index("roll")
    row = lax.axis_index("rows")
    mine = lax.axis_index("groups") if n_groups == 2 else 0
    sibling = me + 1 - 2 * lax.rem(me, 2)
    half = n_roll // 2
    cwp = w_ref.shape[0]
    width = n_roll * cwp
    slabs, depth, height, dense = lat_ref.shape
    frames = depth - 2
    cols = feat_ref.shape[3]
    lat = dense // cols
    cells = height * cols
    feats = gain_ref.shape[1]
    total = n_rows * cells
    chunk = w_ref.shape[1] // 3
    part = chunk // n_groups if n_groups == 2 else chunk

    barrier = pltpu.get_barrier_semaphore()
    for s in range(1, n_rows):
        pl.semaphore_signal(barrier, inc=1, device_id={"rows": lax.rem(row + s, n_rows)},
                            device_id_type=pl.DeviceIdType.MESH)
    for s in range(1, half):
        pl.semaphore_signal(barrier, inc=1, device_id={"roll": lax.rem(me + 2 * s, n_roll)},
                            device_id_type=pl.DeviceIdType.MESH)
    pl.semaphore_signal(barrier, inc=1, device_id={"roll": sibling},
                        device_id_type=pl.DeviceIdType.MESH)
    if n_groups == 2:
        pl.semaphore_signal(barrier, inc=1, device_id={"groups": 1 - mine},
                            device_id_type=pl.DeviceIdType.MESH)
    wes[...] = jnp.zeros_like(wes)
    for a in range(3):
        for b in range(3):
            k0 = (a * 3 + b) * 3 * lat
            wes[b, a * dense // 2:a * dense // 2 + 3 * lat] = ew_ref[k0:k0 + 3 * lat]
    pl.semaphore_wait(barrier, n_rows - 1 + half + (n_groups == 2))

    def piece(ref, a):
        return ref.at[:, pl.ds(a * chunk, chunk)]

    def lat_copy(s):
        return remote(lat_ref, lg.at[row], lsend.at[s], lrecv.at[s], "rows", lax.rem(row + s, n_rows))

    def hop(k, way):
        src = lax.rem(row - way * k + n_rows, n_rows)
        to = lax.rem(row + way + n_rows, n_rows)
        d = 0 if way > 0 else 1
        return remote(feat_ref if k == 0 else fg.at[src], fg.at[src],
                      gsend.at[d, k], grecv.at[d, k], "rows", to)

    def sends(k, way):
        if way > 0:
            return (row >= k) & (row < n_rows - 1)
        return (row + k < n_rows) & (row > 0)

    def receives(k, way):
        return row > k if way > 0 else row + k + 1 < n_rows

    def relay(k):
        for way in (1, -1):
            if k > 0:
                @pl.when(receives(k - 1, way))
                def _():
                    hop(k - 1, way).wait_recv()
            if k < n_rows - 1:
                @pl.when(sends(k, way))
                def _():
                    hop(k, way).start()

    def share(ref, a, h):
        return ref.at[:, pl.ds(pl.multiple_of(a * chunk + h * part, LANES), part)]

    def direct(s, a):
        return remote(share(w_ref, a, mine), share(wg.at[me], a, mine), wsend.at[s, a],
                      wrecv.at[s, a], "roll", lax.rem(me + 2 * s, n_roll))

    def slot_of(s):
        return lax.rem(me - 2 * s + n_roll, n_roll)

    def swap(s, a):
        block = share(wg.at[slot_of(s)], a, mine)
        return remote(block, block, xsend.at[s, a], xrecv.at[s, a], "groups", 1 - mine)

    def give(a):
        return remote(piece(w_ref, a), piece(wg.at[me], a), fsend.at[0, 0, a], frecv.at[0, 0, a],
                      "roll", sibling)

    def forward(s, a, u):
        block = share(wg.at[slot_of(s)], a, mine if u == 0 else 1 - mine)
        return remote(block, block, fsend.at[u, s, a], frecv.at[u, s, a], "roll", sibling)

    own = [
        pltpu.make_async_copy(lat_ref, lg.at[row], own_sem.at[0]),
        pltpu.make_async_copy(feat_ref, fg.at[row], own_sem.at[1]),
        pltpu.make_async_copy(w_ref, wg.at[me], own_sem.at[2]),
    ]
    for c in own:
        c.start()
    for s in range(1, n_rows):
        lat_copy(s).start()
    relay(0)
    for a in (2, 1, 0):
        for s in range(1, half):
            direct(s, a).start()
        give(a).start()

    def pass_on(a):
        for s in range(1, half):
            direct(s, a).wait_recv()
            if n_groups == 2:
                swap(s, a).start()
            forward(s, a, 0).start()

    def pass_swap(a):
        if n_groups == 2:
            for s in range(1, half):
                swap(s, a).wait_recv()
                forward(s, a, 1).start()

    own[0].wait()
    for s in range(1, n_rows):
        lat_copy(s).wait_recv()

    lane = lax.broadcasted_iota(jnp.int32, (8, feats), 1)
    sub = lax.broadcasted_iota(jnp.int32, (8, feats), 0)
    column = lax.rem(lax.broadcasted_iota(jnp.int32, (total, feats), 0), cols)
    group = feats // GROUPS
    count = float(total * group)
    high = n_rows * height
    at = lax.broadcasted_iota(jnp.int32, (high, cols, dense), 1)
    place = lax.broadcasted_iota(jnp.int32, (high, cols, dense), 2)
    keep = (place < 3 * lat) & ((at > 0) | (place >= lat)) & ((at < cols - 1) | (place < 2 * lat))

    def expand(i, carry):
        s, f = i // depth, lax.rem(i, depth)
        r = jnp.concatenate([lg[z, s, f].astype(jnp.float32) for z in range(n_rows)], axis=0)
        x = jnp.zeros((high, cols, dense), jnp.float32)
        for j in range(cols):
            move = (dense - lat * (j - 1)) % dense
            rj = pltpu.roll(r, move, 1) if move else r
            x = jnp.where(at == j, rj[:, None, :], x)
        x = jnp.where(keep & ((f >= 2) | (starts_ref[s] > 0)), x, 0.0)
        xs[s, f] = x.reshape(total, dense)
        return carry

    lax.fori_loop(0, slabs * depth, expand, 0)

    def spread(s, f, start, v, col):
        size = v.shape[0]
        rows = pl.ds(start, size)
        xc[s, 1, f, rows, :] = v.astype(jnp.bfloat16)
        xc[s, 0, f, rows, :] = jnp.where(col == 0, 0.0, pltpu.roll(v, 1, 0)).astype(jnp.bfloat16)
        xc[s, 2, f, rows, :] = jnp.where(
            col == cols - 1, 0.0, pltpu.roll(v, size - 1, 0)).astype(jnp.bfloat16)

    def entry(i, carry):
        s, t = i // frames, lax.rem(i, frames)
        p = jnp.concatenate(
            [xs[s, t] + pltpu.roll(xs[s, t + 1], dense // 2, 1), xs[s, t + 2]], axis=1
        ).astype(jnp.bfloat16)
        ys = [jnp.dot(p, wes[b], preferred_element_type=jnp.float32) for b in range(3)]
        zero = jnp.zeros((cols, feats), jnp.float32)
        h = (ys[1] + jnp.concatenate([zero, ys[0][:-cols]], axis=0)
             + jnp.concatenate([ys[2][cols:], zero], axis=0))
        hid[s, t] = h
        first = jnp.sum(h, axis=0, keepdims=True)
        second = jnp.sum(h * h, axis=0, keepdims=True)
        both = jnp.where(sub == 0, first, second)
        k = 1
        while k < group:
            other = jnp.where((lane // k) % 2 == 1, pltpu.roll(both, k, 1),
                              pltpu.roll(both, feats - k, 1))
            both = both + other
            k *= 2
        both = both / count
        mean, square = both[0:1], both[1:2]
        scaled = lax.rsqrt(square - mean * mean + EPSILON)
        v = (h - mean) * scaled * gain_ref[...] + shift_ref[...]
        v = v / (1.0 + jnp.exp(-v))
        spread(s, 2 + t, 0, v, column)
        return carry

    jobs = slabs * frames
    lax.fori_loop(0, jobs // 3, entry, 0)
    pass_on(2)
    lax.fori_loop(jobs // 3, 2 * jobs // 3, entry, 0)
    relay(1)
    pass_on(1)
    pass_swap(2)
    lax.fori_loop(2 * jobs // 3, jobs, entry, 0)
    pass_on(0)
    pass_swap(1)
    own[2].wait()

    def arrive(a):
        give(a).wait_recv()
        for s in range(1, half):
            forward(s, a, 0).wait_recv()
            if n_groups == 2:
                forward(s, a, 1).wait_recv()

    def taps(a, s, t0, t1):
        y = None
        for c in range(3):
            x = xc[s, c, a + t0:a + t1].reshape((t1 - t0) * total, feats)
            parts = []
            for b in range(3):
                k0 = ((a * 3 + b) * 3 + c) * feats
                parts.append(wg[:, :, k0:k0 + feats].reshape(width, feats))
            wmat = jnp.concatenate(parts, axis=0)
            d = lax.dot_general(x, wmat, (((1,), (1,)), ((), ())),
                                preferred_element_type=jnp.float32)
            y = d if y is None else y + d
        rows = slice(t0 * total, t1 * total)
        acc[s, rows] = y if a == 2 else acc[s, rows] + y

    def each(a, t0, t1):
        def body(s, carry):
            taps(a, s, t0, t1)
            return carry
        lax.fori_loop(0, slabs, body, 0)

    relay(2)
    arrive(2)
    for s in range(slabs):
        taps(2, s, 0, frames)
        if s == 0:
            pass_swap(0)
    arrive(1)
    each(1, 1, frames)
    arrive(0)

    span = n_rows * cw
    tile_lane = lax.broadcasted_iota(jnp.int32, (total, LANES), 1)

    def finish(s, t):
        rows = pl.ds(t * total, total)
        y = [acc[s, rows, b * width:(b + 1) * width] for b in range(3)]
        zero = jnp.zeros((cols, width), jnp.float32)
        m = (y[1] + jnp.concatenate([zero, y[0][:-cols]], axis=0)
             + jnp.concatenate([y[2][cols:], zero], axis=0))
        tiles = []
        for q in range(width // LANES):
            base = jnp.zeros((total, LANES), jnp.float32)
            for r in range(q * LANES // cwp, (q + 1) * LANES // cwp):
                tile = (r * span) // LANES
                offset = (r * span) % LANES + row * cw
                put = r * cwp - q * LANES
                h = hid[s, t, :, tile * LANES:(tile + 1) * LANES]
                h = pltpu.roll(h, lax.rem(put - offset + 2 * LANES, LANES), 1)
                base = jnp.where((tile_lane >= put) & (tile_lane < put + cw), h, base)
            tiles.append(base)
        hc = jnp.concatenate(tiles, axis=1) if len(tiles) > 1 else tiles[0]
        live = (plan_ref[s] >= 0) & (t < lengths_ref[s])
        o = jnp.where(live, m + hc, 0.0).astype(jnp.bfloat16)
        for z in range(n_rows):
            res[s, z, t] = o[z * cells:(z + 1) * cells]

    def late(u):
        return pl.ds(2, frames - 2) if u == 0 else pl.ds(0, 2)

    def result(s, u, k):
        to = lax.rem(row + k, n_rows)
        return remote(res.at[s, to, late(u)], got.at[s, row, late(u)],
                      rsend.at[s, u, k], rrecv.at[s, u, k], "rows", to)

    def close(s, u):
        for t in range(2, frames) if u == 0 else range(2):
            finish(s, t)
        for k in range(1, n_rows):
            result(s, u, k).start()
        got[s, row, late(u)] = res[s, row, late(u)]

    for s in range(slabs):
        taps(0, s, 2, frames)
        close(s, 0)

    for k in range(3, n_rows):
        relay(k)
    own[1].wait()

    def cache(i, carry):
        s, f = i // 2, lax.rem(i, 2)
        for z in range(n_rows):
            v = fg[z, s, f].astype(jnp.float32).reshape(cells, feats)
            v = jnp.where(starts_ref[s] > 0, v, 0.0)
            spread(s, f, z * cells, v, column[:cells])
        return carry

    lax.fori_loop(0, slabs * 2, cache, 0)
    for s in range(slabs):
        taps(1, s, 0, 1)
        taps(0, s, 0, 2)
        close(s, 1)

    owner_lane = lax.broadcasted_iota(jnp.int32, (cells, LANES), 1)

    def placed(s, t):
        tiles = [jnp.zeros((cells, LANES), jnp.float32) for _ in range(feats // LANES)]
        for z in range(n_rows):
            g = got[s, z, t].astype(jnp.float32)
            for r in range(n_roll):
                q, take = (r * cwp) // LANES, (r * cwp) % LANES
                start = (r * n_rows + z) * cw
                tile, put = start // LANES, start % LANES
                h = g[:, q * LANES:(q + 1) * LANES]
                move = (put - take) % LANES
                if move:
                    h = pltpu.roll(h, move, 1)
                tiles[tile] = jnp.where(
                    (owner_lane >= put) & (owner_lane < put + cw), h, tiles[tile])
        o = jnp.concatenate(tiles, axis=1)
        out_ref[s, t] = o.reshape(height, cols, feats).astype(jnp.bfloat16)

    for u in range(2):
        for s in range(slabs):
            for k in range(1, n_rows):
                result(s, u, k).wait_recv()

            def gather(t, carry, s=s):
                placed(s, t)
                return carry

            lax.fori_loop(2 if u == 0 else 0, frames if u == 0 else 2, gather, 0)

    for s in range(1, n_rows):
        lat_copy(s).wait_send()
        for i in range(slabs):
            for u in range(2):
                result(i, u, s).wait_send()
    for k in range(n_rows - 1):
        for way in (1, -1):
            @pl.when(sends(k, way))
            def _():
                hop(k, way).wait_send()
    for a in range(3):
        give(a).wait_send()
        for s in range(1, half):
            direct(s, a).wait_send()
            forward(s, a, 0).wait_send()
            if n_groups == 2:
                swap(s, a).wait_send()
                forward(s, a, 1).wait_send()


def on_device(
    latent_slabs, prior_latents, prior_features, lengths, starts, move_plan,
    entry_weight, block_weight, norm_gain, norm_shift,
):
    n_roll, n_rows = lax.axis_size("roll"), lax.axis_size("rows")
    slabs, frames, height, cols, lat = latent_slabs.shape
    feats = prior_features.shape[-1]
    cells = height * cols
    total = cells * n_rows
    dense = cols * lat
    cw = block_weight.shape[1]
    cwp = max(cw, 16)
    width = n_roll * cwp
    dense_lat = jnp.concatenate([prior_latents, latent_slabs], axis=1).reshape(
        slabs, frames + 2, height, dense)
    wt = block_weight.T
    if cwp != cw:
        wt = jnp.pad(wt, ((0, cwp - cw), (0, 0)))
    vm = pl.BlockSpec(memory_space=pltpu.VMEM)
    sm = pl.BlockSpec(memory_space=pltpu.SMEM)
    hbm = pl.BlockSpec(memory_space=pl.ANY)
    half = n_roll // 2
    dma = pltpu.SemaphoreType.DMA
    return pl.pallas_call(
        functools.partial(kernel, lax.axis_size("groups"), n_roll, n_rows, cw),
        out_shape=jax.ShapeDtypeStruct((slabs, frames, height, cols, feats), jnp.bfloat16),
        in_specs=[sm] * 3 + [hbm, vm, hbm] + [vm] * 3,
        out_specs=vm,
        scratch_shapes=[
            pltpu.VMEM((n_roll, cwp, wt.shape[1]), jnp.bfloat16),
            pltpu.VMEM((n_rows, slabs, frames + 2, height, dense), jnp.bfloat16),
            pltpu.VMEM((n_rows, slabs, 2, height, cols, feats), jnp.bfloat16),
            pltpu.VMEM((3, 2 * dense, feats), jnp.bfloat16),
            pltpu.VMEM((slabs, frames + 2, total, dense), jnp.float32),
            pltpu.VMEM((slabs, frames, total, feats), jnp.float32),
            pltpu.VMEM((slabs, 3, frames + 2, total, feats), jnp.bfloat16),
            pltpu.VMEM((slabs, frames * total, 3 * width), jnp.float32),
            pltpu.VMEM((slabs, n_rows, frames, cells, width), jnp.bfloat16),
            pltpu.VMEM((slabs, n_rows, frames, cells, width), jnp.bfloat16),
            dma((3,)),
            dma((half, 3)), dma((half, 3)), dma((half, 3)), dma((half, 3)),
            dma((2, half, 3)), dma((2, half, 3)),
            dma((n_rows,)), dma((n_rows,)),
            dma((2, n_rows)), dma((2, n_rows)),
            dma((slabs, 2, n_rows)), dma((slabs, 2, n_rows)),
        ],
        compiler_params=pltpu.CompilerParams(
            collective_id=0, has_side_effects=True, vmem_limit_bytes=67043328
        ),
        name="decode",
    )(
        lengths, starts, move_plan, wt, dense_lat, prior_features, entry_weight,
        norm_gain[None], norm_shift[None],
    )


def solution(mesh):
    in_specs = (
        P(("groups", "roll"), None, "rows", None, None),
        P(("groups", "roll"), None, "rows", None, None),
        P(("groups", "roll"), None, "rows", None, None),
        P(("groups", "roll")),
        P(("groups", "roll")),
        P(("groups", "roll")),
        P(),
        P(None, ("roll", "rows")),
        P(),
        P(),
    )
    out_specs = P(("groups", "roll"), None, "rows", None, None)
    return jax.shard_map(
        on_device, mesh=mesh, in_specs=in_specs, out_specs=out_specs, check_vma=False
    )
```
